32 devices in a mesh: ctx: 8 (over z, core), head: 4 (over y, x).
Axes of the slice: x: 2, y: 2, z: 4, core: 2. Of those that a mesh axis runs over, the one named last changes fastest.
Arguments:
- ssd_input: bfloat16 [4096, 4096], P('ctx', 'head'), may hold values from -0.29882812 to 0.29882812
- log_decay: float32 [64, 4096], P('head', 'ctx'), may hold values from -2.5 to 0
- write_proj: bfloat16 [4096, 4, 128], P('ctx', 'head'), may hold values from -0.23925781 to 0.23925781
- read_proj: bfloat16 [4096, 4, 128], P('ctx', 'head'), may hold values from -0.23925781 to 0.23925781
- in_weight: bfloat16 [4096, 4096], P(None, 'head'), may hold values from -0.125 to 0.125
- out_weight: bfloat16 [4096, 4096], P('head'), may hold values from -0.125 to 0.125
- out_grad: bfloat16 [4096, 4096], P('ctx', 'head'), may hold values from -6 to 6
Outputs:
- input_grad: bfloat16 [4096, 4096], P('ctx', 'head')
- write_grad: float32 [4096, 4, 128], P('ctx', 'head')
- read_grad: float32 [4096, 4, 128], P('ctx', 'head')
The draws below stay inside these ranges and needn't reach their ends.
All inputs are finite; a program needn't handle non-finite values.
Results may differ from the reference program's by a relative error of at most 0.017.
Values may be sent and summed in bfloat16 or wider, within the bound.
A program may use at most 128 MiB of HBM per device.

```python
import jax
import jax.numpy as jnp
from jax import lax

D = 4096
HEADS_DEV = 16
P_SIZE = 64
N = 128
SPAN = 256
TOK_DEV = 512
HEADS = 64
GROUPS = 4
TOKEN_POSITIONS = 4096


def draw_log_decay(key, part):
    random_key_list = jax.random.split(jax.random.fold_in(key, 17), 9)
    fast_share = 0.5
    quick = jax.random.uniform(random_key_list[0], (HEADS,)) < fast_share
    fast = jnp.exp(jax.random.uniform(random_key_list[1], (HEADS,), minval=jnp.log(0.06), maxval=jnp.log(0.35)))
    slow = 0.4 / TOKEN_POSITIONS * jnp.exp(jax.random.uniform(random_key_list[2], (HEADS,), minval=-0.7, maxval=0.7))
    random_noise = jnp.exp(jax.random.uniform(random_key_list[3], (HEADS, TOKEN_POSITIONS), minval=-0.7, maxval=0.7))
    blocks = jnp.exp(jax.random.uniform(random_key_list[4], (HEADS, TOKEN_POSITIONS // SPAN), minval=-0.7, maxval=0.7))
    block_multiplier = jnp.repeat(blocks, SPAN, axis=1)
    stretch = SPAN // 8
    active = jax.random.uniform(random_key_list[7], (HEADS, TOKEN_POSITIONS // stretch)) < 0.5
    stretch_factor = jnp.repeat(jnp.where(active, 1.0, 0.001), stretch, axis=1)
    resting = jax.random.uniform(random_key_list[8], (HEADS, TOKEN_POSITIONS // TOK_DEV)) < 0.4
    device_factor = jnp.repeat(jnp.where(resting, 0.001, 1.0), TOK_DEV, axis=1)
    fast_rate = fast[:, None] * stretch_factor * device_factor
    decay_speed = jnp.where(quick[:, None], fast_rate, slow[:, None])
    position_table = jax.random.randint(random_key_list[5], (3,), 0, TOKEN_POSITIONS)
    spike_magnitude = jax.random.uniform(random_key_list[6], (3,), minval=0.22, maxval=0.69)
    spike_total_sum = jnp.sum(jnp.where(jnp.arange(TOKEN_POSITIONS)[None, :] == position_table[:, None], spike_magnitude[:, None], 0.0), axis=0)
    return (-(decay_speed * random_noise * block_multiplier) - spike_total_sum[None, :]).astype(jnp.float32)


def strengthened(array, key, source, target, blocks, factor):
    def block_of(dim):
        return (jnp.arange(array.shape[dim]) // (array.shape[dim] // blocks)).reshape((-1,) + (1,) * (array.ndim - 1 - dim))

    near = jax.random.permutation(key, blocks)[block_of(target)]
    other_side = (block_of(target) + blocks // 2) % blocks
    return jnp.where((block_of(source) == near) | (block_of(source) == other_side), factor * array, array)


def block_levels(key, dims, cuts, smallest, high):
    def one(axis_at, blocks):
        draws = jax.random.uniform(jax.random.fold_in(jax.random.fold_in(key, 6), axis_at), (blocks,), jnp.float32, smallest / len(cuts), high / len(cuts))
        return jnp.repeat(jnp.exp(draws), dims[axis_at] // blocks).reshape((-1,) + (1,) * (len(dims) - axis_at - 1))

    gain = one(*cuts[0])
    for cut in cuts[1:]:
        gain = gain * one(*cut)
    return gain


def centred(own_key, shape, width, most, cuts=(), kind=jnp.bfloat16):
    array = width * jax.random.normal(own_key, shape, jnp.float32)
    if cuts:
        array = array * block_levels(own_key, shape, cuts, -0.22, 0.18)
    return jnp.clip(array, -most, most).astype(kind)


def gaussian_with(own_key, shape, spread, bound, shards, heavy, kind=jnp.bfloat16):
    array = spread * jax.random.normal(own_key, shape, jnp.float32)
    if shards:
        array = array * block_levels(own_key, shape, shards, -0.22, 0.18)
    return jnp.clip(strengthened(array, jax.random.fold_in(own_key, 3), *heavy), -bound, bound).astype(kind)


def setup_inputs(seed: int = 0) -> dict:
    seeds = jax.random.split(jax.random.key(seed), 8)
    ssd_input = centred(seeds[0], (TOKEN_POSITIONS, HEADS * P_SIZE), 0.05, 0.29882812, ((0, 8), (1, 4)))
    log_decay = draw_log_decay(jax.random.fold_in(seeds[7], 71), 0)
    write_proj = centred(seeds[2], (TOKEN_POSITIONS, GROUPS, N), 0.04, 0.23925781, ((0, 8), (1, 4)))
    read_proj = centred(seeds[3], (TOKEN_POSITIONS, GROUPS, N), 0.04, 0.23925781, ((0, 8), (1, 4)))
    in_weight = gaussian_with(seeds[4], (D, HEADS * P_SIZE), D ** -0.5, 0.125, ((1, 4),), (1, 0, 4, 2.0))
    out_weight = gaussian_with(seeds[5], (HEADS * P_SIZE, D), (HEADS * P_SIZE) ** -0.5, 0.125, ((0, 4),), (1, 0, 4, 2.0))
    out_grad = centred(seeds[6], (TOKEN_POSITIONS, D), 1.0, 6.0, ((0, 8), (1, 4)))
    return dict(ssd_input=ssd_input, log_decay=log_decay, write_proj=write_proj, read_proj=read_proj, in_weight=in_weight, out_weight=out_weight, out_grad=out_grad)


HIGH = lax.Precision.HIGHEST


def reference(ssd_input, log_decay, write_proj, read_proj, in_weight, out_weight, out_grad):
    out_step = jnp.dot(out_grad, out_weight.T, preferred_element_type=jnp.float32).astype(jnp.bfloat16)
    nchunk = TOKEN_POSITIONS // SPAN
    xs = ssd_input.reshape(nchunk, SPAN, HEADS, P_SIZE)
    dys = out_step.reshape(nchunk, SPAN, HEADS, P_SIZE)
    writes = write_proj.reshape(nchunk, SPAN, GROUPS, N)
    reads = read_proj.reshape(nchunk, SPAN, GROUPS, N)
    decays = jnp.transpose(log_decay.reshape(HEADS, nchunk, SPAN), (1, 0, 2))
    group_of = (jnp.arange(HEADS) // HEADS_DEV).astype(jnp.int32)
    order = lax.broadcasted_iota(jnp.int32, (SPAN, SPAN), 0) >= lax.broadcasted_iota(jnp.int32, (SPAN, SPAN), 1)

    def group_sum(per_head):
        return per_head.reshape(SPAN, GROUPS, HEADS_DEV, N).sum(axis=2)

    def forward_stretch(state, pieces):
        xq, dq, wq, rq, lq = pieces
        xq = xq.astype(jnp.float32)
        dq = dq.astype(jnp.float32)
        wh = wq.astype(jnp.float32)[:, group_of, :]
        rh = rq.astype(jnp.float32)[:, group_of, :]
        cumul = jnp.cumsum(lq, axis=1)
        diff = cumul[:, :, None] - cumul[:, None, :]
        decay = jnp.where(order[None], jnp.exp(jnp.where(order[None], diff, 0.0)), 0.0)
        scores = jnp.einsum("shn,thn->hst", rh, wh, precision=HIGH)
        mixed = jnp.einsum("thp,shp->hts", dq, xq, precision=HIGH)
        weight = decay * mixed
        read_h = jnp.einsum("hts,shn->thn", weight, wh, precision=HIGH)
        write_h = jnp.einsum("hst,shn->thn", weight, rh, precision=HIGH)
        input_intra = jnp.einsum("hst,shp->thp", decay * scores, dq, precision=HIGH)
        grow = jnp.exp(cumul)
        read_h = read_h + jnp.einsum("ht,thp,hpn->thn", grow, dq, state, precision=HIGH)
        fade = jnp.exp(cumul[:, -1:] - cumul)
        ending = jnp.einsum("hs,shp,shn->hpn", fade, xq, wh, precision=HIGH)
        state = jnp.exp(cumul[:, -1])[:, None, None] * state + ending
        return state, (input_intra, group_sum(read_h), group_sum(write_h))

    def backward_stretch(carry, pieces):
        xq, dq, wq, rq, lq = pieces
        xq = xq.astype(jnp.float32)
        dq = dq.astype(jnp.float32)
        wh = wq.astype(jnp.float32)[:, group_of, :]
        rh = rq.astype(jnp.float32)[:, group_of, :]
        cumul = jnp.cumsum(lq, axis=1)
        fade = jnp.exp(cumul[:, -1:] - cumul)
        grow = jnp.exp(cumul)
        input_inter = jnp.einsum("ht,hpn,thn->thp", fade, carry, wh, precision=HIGH)
        write_h = jnp.einsum("ht,hpn,thp->thn", fade, carry, xq, precision=HIGH)
        leaving = jnp.einsum("hs,shp,shn->hpn", grow, dq, rh, precision=HIGH)
        carry = leaving + jnp.exp(cumul[:, -1])[:, None, None] * carry
        return carry, (input_inter, group_sum(write_h))

    zeros = jnp.zeros((HEADS, P_SIZE, N), jnp.float32)
    pieces = (xs, dys, writes, reads, decays)
    _, (input_intra, read_parts, write_intra) = lax.scan(forward_stretch, zeros, pieces)
    _, (input_inter, write_inter) = lax.scan(backward_stretch, zeros, pieces, reverse=True)
    x_grad = (input_intra + input_inter).reshape(TOKEN_POSITIONS, HEADS * P_SIZE).astype(jnp.bfloat16)
    input_grad = jnp.dot(x_grad, in_weight.T, preferred_element_type=jnp.float32).astype(jnp.bfloat16)
    write_grad = (write_intra + write_inter).reshape(TOKEN_POSITIONS, GROUPS, N)
    read_grad = read_parts.reshape(TOKEN_POSITIONS, GROUPS, N)
    return input_grad, write_grad, read_grad
```

```python
import functools

import jax
import jax.numpy as jnp
from jax import lax
from jax.experimental import pallas as pl
from jax.experimental.pallas import tpu as pltpu
from jax.sharding import PartitionSpec as P

CHUNK = 128
SUB = 2
MESH = pl.DeviceIdType.MESH
HIGH = lax.Precision.HIGHEST
F32 = jnp.float32
BF16 = jnp.bfloat16
NT = (((1,), (1,)), ((), ()))
TN = (((0,), (0,)), ((), ()))
VMEM_LIMIT = 60 * 1024 * 1024


def mm(a, b, dims=(((1,), (0,)), ((), ())), precision=None):
    return lax.dot_general(a, b, dims, precision=precision, preferred_element_type=F32)


def ring_index(place, n):
    half = n // 2
    return jnp.where(place < half, place, n + half - 1 - place)


def greet(axis, targets):
    barrier = pltpu.get_barrier_semaphore()
    for target in targets:
        pl.semaphore_signal(barrier, inc=1, device_id={axis: target}, device_id_type=MESH)
    pl.semaphore_wait(barrier, len(targets))


def gather_kernel(n, x_ref, w_ref, dy_ref, buf, wv, acc, wsem, ssem, rsem):
    rows, feats = x_ref.shape
    width = w_ref.shape[0]
    me = lax.axis_index("head")
    place = ring_index(me, n)
    right = ring_index(lax.rem(place + 1, n), n)
    left = ring_index(lax.rem(place + n - 1, n), n)
    half = rows // 2
    piece = half // SUB
    greet("head", (left, right))

    def span(d, g):
        return pl.ds(d * half + g * piece, piece)

    def copy(s, d, g):
        src = x_ref.at[span(d, g)] if s == 0 else buf.at[s - 1, span(d, g)]
        return pltpu.make_async_remote_copy(
            src_ref=src,
            dst_ref=buf.at[s, span(d, g)],
            send_sem=ssem.at[s, d, g],
            recv_sem=rsem.at[s, d, g],
            device_id={"head": right if d == 0 else left},
            device_id_type=MESH,
        )

    def owner(s, d):
        return ring_index(lax.rem(place + (n - s if d == 0 else s), n), n)

    for g in range(SUB):
        for d in range(2):
            copy(0, d, g).start()

    def weight(b):
        at = pl.multiple_of(b * feats, 128)
        return pltpu.make_async_copy(w_ref.at[:, pl.ds(at, feats)], wv.at[b], wsem.at[b])

    for b in range(n):
        weight(b).start()
    for b in range(n):
        weight(b).wait()

    tile = 256

    def accumulate(s, d, row0, count):
        own = owner(s, d)
        src = x_ref if s == 0 else buf.at[s - 1]

        @pl.loop(0, width // tile)
        def _(j):
            cols = pl.ds(pl.multiple_of(j * tile, tile), tile)
            part = mm(src[pl.ds(row0, count), :], wv[own, cols, :], NT)
            at = (pl.ds(row0, count), cols)
            if s == 0:
                acc[at] = part
            elif s == n - 1:
                dy_ref[at] = (acc[at] + part).astype(dy_ref.dtype)
            else:
                acc[at] += part

    for s in range(n - 1):
        if s > 0:
            for g in range(SUB):
                for d in range(2):
                    copy(s - 1, d, g).wait_recv()
                    copy(s, d, g).start()
        for d in range(2):
            accumulate(s, d, d * half, half)
    for g in range(SUB):
        for d in range(2):
            copy(n - 2, d, g).wait_recv()
            accumulate(n - 1, d, d * half + g * piece, piece)
    for s in range(n - 1):
        for g in range(SUB):
            for d in range(2):
                copy(s, d, g).wait_send()


def gather_product(n, grad, weight):
    rows, feats = grad.shape
    width = weight.shape[0]
    return pl.pallas_call(
        functools.partial(gather_kernel, n),
        name="gather_product",
        out_shape=jax.ShapeDtypeStruct((rows, width), BF16),
        in_specs=[
            pl.BlockSpec(memory_space=pltpu.VMEM),
            pl.BlockSpec(memory_space=pl.ANY),
        ],
        out_specs=pl.BlockSpec(memory_space=pltpu.VMEM),
        scratch_shapes=[
            pltpu.VMEM((n - 1, rows, feats), BF16),
            pltpu.VMEM((n, width, feats), BF16),
            pltpu.VMEM((rows, width), F32),
            pltpu.SemaphoreType.DMA((n,)),
            pltpu.SemaphoreType.DMA((n - 1, 2, SUB)),
            pltpu.SemaphoreType.DMA((n - 1, 2, SUB)),
        ],
        compiler_params=pltpu.CompilerParams(
            collective_id=0, has_side_effects=True, vmem_limit_bytes=VMEM_LIMIT
        ),
    )(grad, weight)


def scatter_kernel(n, x_ref, w_ref, out_ref, wv, rbuf, sbuf, wsem, ssem, rsem):
    rows, depth = x_ref.shape
    cols = out_ref.shape[1]
    me = lax.axis_index("head")
    place = ring_index(me, n)
    right = ring_index(lax.rem(place + 1, n), n)
    left = ring_index(lax.rem(place + n - 1, n), n)
    half = rows // 2
    piece = half // SUB

    def weight(b):
        return pltpu.make_async_copy(w_ref.at[pl.ds(b * cols, cols)], wv.at[b], wsem.at[b])

    for b in range(n):
        weight(b).start()
    greet("head", (left, right))
    for b in range(n):
        weight(b).wait()

    def copy(s, d, g):
        at = pl.ds(d * half + g * piece, piece)
        return pltpu.make_async_remote_copy(
            src_ref=sbuf.at[s, at],
            dst_ref=rbuf.at[s, at],
            send_sem=ssem.at[s, d, g],
            recv_sem=rsem.at[s, d, g],
            device_id={"head": right if d == 0 else left},
            device_id_type=MESH,
        )

    tile = 256

    def term(s, d, g):
        if d == 0:
            dest = ring_index(lax.rem(place + 2 * n - 1 - s, n), n)
        else:
            dest = ring_index(lax.rem(place + 1 + s, n), n)
        at = pl.ds(d * half + g * piece, piece)

        @pl.loop(0, cols // tile)
        def _(j):
            lanes = pl.ds(pl.multiple_of(j * tile, tile), tile)
            part = mm(x_ref[at, :], wv[dest, lanes, :], NT)
            if s > 0:
                part = part + rbuf[s - 1, at, lanes].astype(F32)
            if s == n - 1:
                out_ref[at, lanes] = part.astype(out_ref.dtype)
            else:
                sbuf[s, at, lanes] = part.astype(BF16)

    for s in range(n):
        for g in range(SUB):
            for d in range(2):
                if s > 0:
                    copy(s - 1, d, g).wait_recv()
                term(s, d, g)
                if s < n - 1:
                    copy(s, d, g).start()
    for s in range(n - 1):
        for g in range(SUB):
            for d in range(2):
                copy(s, d, g).wait_send()


def product_scatter(n, x_grad, weight):
    rows, depth = x_grad.shape
    cols = weight.shape[0] // n
    return pl.pallas_call(
        functools.partial(scatter_kernel, n),
        name="product_scatter",
        out_shape=jax.ShapeDtypeStruct((rows, cols), BF16),
        in_specs=[
            pl.BlockSpec(memory_space=pltpu.VMEM),
            pl.BlockSpec(memory_space=pl.ANY),
        ],
        out_specs=pl.BlockSpec(memory_space=pltpu.VMEM),
        scratch_shapes=[
            pltpu.VMEM((n, cols, depth), BF16),
            pltpu.VMEM((n - 1, rows, cols), BF16),
            pltpu.VMEM((n - 1, rows, cols), BF16),
            pltpu.SemaphoreType.DMA((n,)),
            pltpu.SemaphoreType.DMA((n - 1, 2, SUB)),
            pltpu.SemaphoreType.DMA((n - 1, 2, SUB)),
        ],
        compiler_params=pltpu.CompilerParams(
            collective_id=1, has_side_effects=True, vmem_limit_bytes=VMEM_LIMIT
        ),
    )(x_grad, weight)


PIECES = 4
POINTS = 2


def state_kernel(
    n, x_ref, ld_ref, b_ref, c_ref, dy_ref, xg_ref, wg_ref, rg_ref,
    ends, leaves, grown, faded, fades, intra, lrow, lcol, etot, wacc,
    end_own, leave_own, s_in, s_out, g_in, g_out, sem_ss, sem_sr, sem_gs, sem_gr,
):
    rows, width = x_ref.shape
    heads = ld_ref.shape[0]
    nstate = b_ref.shape[1]
    hp = width // heads
    q = CHUNK
    nc = rows // q
    pairs = heads // 2
    me = lax.axis_index("ctx")
    ahead = jnp.minimum(me + 1, n - 1)
    behind = jnp.maximum(me - 1, 0)

    barrier = pltpu.get_barrier_semaphore()

    @pl.when(me < n - 1)
    def _():
        pl.semaphore_signal(barrier, inc=1, device_id={"ctx": ahead}, device_id_type=MESH)

    @pl.when(me > 0)
    def _():
        pl.semaphore_signal(barrier, inc=1, device_id={"ctx": behind}, device_id_type=MESH)

    pl.semaphore_wait(barrier, jnp.where(me > 0, 1, 0) + jnp.where(me < n - 1, 1, 0))

    @pl.when(me == 0)
    def _():
        s_in[...] = jnp.zeros_like(s_in)

    @pl.when(me == n - 1)
    def _():
        g_in[...] = jnp.zeros_like(g_in)

    first = lax.broadcasted_iota(jnp.int32, (q, q), 0)
    second = lax.broadcasted_iota(jnp.int32, (q, q), 1)
    upto = (first <= second).astype(F32)
    downto = (first >= second).astype(F32)
    after = (first < second).astype(F32)
    ones = jnp.ones((q, nstate), F32)
    head_at = lax.broadcasted_iota(jnp.int32, (heads, width), 0) * hp
    lane_at = lax.broadcasted_iota(jnp.int32, (heads, width), 1)
    spread = ((lane_at >= head_at) & (lane_at < head_at + hp)).astype(BF16)

    def scaled(factor, state):
        out = factor[:, None, :] * state.reshape(heads, hp, nstate)
        return out.reshape(width, nstate)

    total = jnp.zeros((heads, nstate), F32)
    for k in range(nc):
        at = pl.ds(k * q, q)
        ldk = ld_ref[:, k * q : (k + 1) * q]
        lrow[k] = mm(ldk, upto, precision=HIGH)
        cols = mm(downto, ldk, NT, HIGH)
        lcol[k] = cols
        whole = mm(ldk, ones, precision=HIGH)
        total = total + whole
        etot[k] = jnp.exp(whole)
        fade = mm(jnp.exp(mm(after, ldk, NT, HIGH)).astype(BF16), spread)
        grow = mm(jnp.exp(cols).astype(BF16), spread)
        fades[at, :] = fade.astype(BF16)
        fx = (x_ref[at, :].astype(F32) * fade).astype(BF16)
        faded[at, :] = fx
        ends[k] = mm(fx, b_ref[at, :], TN)
        gd = (dy_ref[at, :].astype(F32) * grow).astype(BF16)
        grown[at, :] = gd
        leaves[k] = mm(gd, c_ref[at, :], TN)
    etot[nc] = jnp.exp(total)

    state = ends[0]
    for k in range(1, nc):
        state = scaled(etot[k], state) + ends[k]
    end_own[...] = state
    grad = leaves[nc - 1]
    for k in range(nc - 2, -1, -1):
        grad = leaves[k] + scaled(etot[k], grad)
    leave_own[...] = grad

    hstep = heads // PIECES
    step = width // PIECES

    def relay(own, got, out, sends, recvs, target, receives, passes):
        def copy(i):
            at = pl.ds(i * step, step)
            return pltpu.make_async_remote_copy(
                src_ref=out.at[at],
                dst_ref=got.at[at],
                send_sem=sends.at[i],
                recv_sem=recvs.at[i],
                device_id={"ctx": target},
                device_id_type=MESH,
            )

        def run():
            for i in range(PIECES):
                at = pl.ds(i * step, step)

                @pl.when(receives)
                def _():
                    copy(i).wait_recv()

                @pl.when(passes)
                def _():
                    factor = etot[nc, i * hstep : (i + 1) * hstep, :]
                    come = got[at, :].astype(F32).reshape(hstep, hp, nstate)
                    come = (factor[:, None, :] * come).reshape(step, nstate)
                    out[at, :] = (own[at, :] + come).astype(BF16)
                    copy(i).start()

        def finish():
            @pl.when(passes)
            def _():
                for i in range(PIECES):
                    copy(i).wait_send()

        return run, finish

    run_s, finish_s = relay(end_own, s_in, s_out, sem_ss, sem_sr, ahead, me > 0, me < n - 1)
    run_g, finish_g = relay(leave_own, g_in, g_out, sem_gs, sem_gr, behind, me < n - 1, me > 0)
    points = POINTS * nc
    at_s = (me * points) // n
    at_g = ((n - 1 - me) * points) // n

    low = lax.broadcasted_iota(jnp.int32, (q, 2 * hp), 1) < hp
    keep = jnp.concatenate([first <= second, first <= second], axis=1)

    @pl.loop(0, nc)
    def _(k):
        at = pl.ds(pl.multiple_of(k * q, q), q)
        bk = b_ref[at, :]
        ck = c_ref[at, :]
        score = mm(bk, ck, NT)
        score2 = jnp.concatenate([score, score], axis=1)
        colk = lcol[k]
        for j in range(pairs):
            if j % (pairs // POINTS) == 0:
                point = k * POINTS + j // (pairs // POINTS)
                pl.when(point == at_s)(run_s)
                pl.when(point == at_g)(run_g)
            lanes = slice(j * 2 * hp, (j + 1) * 2 * hp)
            dyp = dy_ref[at, lanes]
            none = jnp.zeros_like(dyp)
            dyst = jnp.concatenate([jnp.where(low, dyp, none), jnp.where(low, none, dyp)], axis=0)
            mixed = mm(x_ref[at, lanes], dyst, NT)
            d0 = lrow[k, 2 * j : 2 * j + 1, :] - colk[:, 2 * j : 2 * j + 1]
            d1 = lrow[k, 2 * j + 1 : 2 * j + 2, :] - colk[:, 2 * j + 1 : 2 * j + 2]
            decay = jnp.exp(jnp.where(keep, jnp.concatenate([d0, d1], axis=1), -1e30))
            if j == 0:
                wacc[...] = decay * mixed
            else:
                wacc[...] += decay * mixed
            intra[at, lanes] = mm((decay * score2).astype(BF16), dyst)
        both = wacc[...]
        weight = (both[:, :q] + both[:, q:]).astype(BF16)
        wg_ref[at, :] = mm(weight, ck)
        rg_ref[at, :] = mm(weight, bk, TN)

    state = s_in[...].astype(F32)
    for k in range(nc):
        at = pl.ds(k * q, q)
        rg_ref[at, :] += mm(grown[at, :], state.astype(BF16))
        if k < nc - 1:
            state = scaled(etot[k], state) + ends[k]
    grad = g_in[...].astype(F32)
    for k in range(nc - 1, -1, -1):
        at = pl.ds(k * q, q)
        gb = grad.astype(BF16)
        inter = mm(b_ref[at, :], gb, NT)
        xg_ref[at, :] = (intra[at, :] + fades[at, :].astype(F32) * inter).astype(BF16)
        wg_ref[at, :] += mm(faded[at, :], gb)
        if k > 0:
            grad = leaves[k] + scaled(etot[k], grad)
    finish_s()
    finish_g()


def state_part(n, x, log_decay, writes, reads, dy):
    rows, width = x.shape
    heads = log_decay.shape[0]
    nstate = writes.shape[1]
    nc = rows // CHUNK
    vm = pl.BlockSpec(memory_space=pltpu.VMEM)
    return pl.pallas_call(
        functools.partial(state_kernel, n),
        name="state_part",
        out_shape=(
            jax.ShapeDtypeStruct((rows, width), BF16),
            jax.ShapeDtypeStruct((rows, nstate), F32),
            jax.ShapeDtypeStruct((rows, nstate), F32),
        ),
        in_specs=[vm] * 5,
        out_specs=(vm, vm, vm),
        scratch_shapes=[
            pltpu.VMEM((nc, width, nstate), F32),
            pltpu.VMEM((nc, width, nstate), F32),
            pltpu.VMEM((rows, width), BF16),
            pltpu.VMEM((rows, width), BF16),
            pltpu.VMEM((rows, width), BF16),
            pltpu.VMEM((rows, width), F32),
            pltpu.VMEM((nc, heads, CHUNK), F32),
            pltpu.VMEM((nc, CHUNK, heads), F32),
            pltpu.VMEM((nc + 1, heads, nstate), F32),
            pltpu.VMEM((CHUNK, 2 * CHUNK), F32),
            pltpu.VMEM((width, nstate), F32),
            pltpu.VMEM((width, nstate), F32),
            pltpu.VMEM((width, nstate), BF16),
            pltpu.VMEM((width, nstate), BF16),
            pltpu.VMEM((width, nstate), BF16),
            pltpu.VMEM((width, nstate), BF16),
            pltpu.SemaphoreType.DMA((PIECES,)),
            pltpu.SemaphoreType.DMA((PIECES,)),
            pltpu.SemaphoreType.DMA((PIECES,)),
            pltpu.SemaphoreType.DMA((PIECES,)),
        ],
        compiler_params=pltpu.CompilerParams(
            collective_id=2, has_side_effects=True, vmem_limit_bytes=VMEM_LIMIT
        ),
    )(x, log_decay, writes, reads, dy)


def per_device(
    nctx, nhead, ssd_input, log_decay, write_proj, read_proj, in_weight, out_weight, out_grad
):
    steps = ssd_input.shape[0]
    nstate = write_proj.shape[2]
    dy = gather_product(nhead, out_grad, out_weight)
    x_grad, write_grad, read_grad = state_part(
        nctx,
        ssd_input,
        log_decay,
        write_proj.reshape(steps, nstate),
        read_proj.reshape(steps, nstate),
        dy,
    )
    input_grad = product_scatter(nhead, x_grad, in_weight)
    return (input_grad, write_grad.reshape(steps, 1, nstate), read_grad.reshape(steps, 1, nstate))


def solution(mesh):
    placed = (
        P("ctx", "head"),
        P("head", "ctx"),
        P("ctx", "head", None),
        P("ctx", "head", None),
        P(None, "head"),
        P("head", None),
        P("ctx", "head"),
    )
    return jax.shard_map(
        functools.partial(per_device, mesh.shape["ctx"], mesh.shape["head"]),
        mesh=mesh,
        in_specs=placed,
        out_specs=(P("ctx", "head"), P("ctx", "head", None), P("ctx", "head", None)),
        check_vma=False,
    )
```

```python
import functools

import jax
import jax.numpy as jnp
from jax import lax
from jax.experimental import pallas as pl
from jax.experimental.pallas import tpu as pltpu
from jax.sharding import PartitionSpec as P

CHUNK = 128
SUB = 2
PIECES = 4
POINTS = 2
TILE = 256
MESH = pl.DeviceIdType.MESH
HIGH = lax.Precision.HIGHEST
F32 = jnp.float32
BF16 = jnp.bfloat16
NT = (((1,), (1,)), ((), ()))
TN = (((0,), (0,)), ((), ()))
VMEM_LIMIT = 60 * 1024 * 1024


def mm(a, b, dims=(((1,), (0,)), ((), ())), precision=None):
    return lax.dot_general(a, b, dims, precision=precision, preferred_element_type=F32)


def ring_index(place, n):
    half = n // 2
    return jnp.where(place < half, place, n + half - 1 - place)


def layer_kernel(
    nctx, nhead, grad_ref, x_hbm, ld_ref, b_ref, c_ref, wo_hbm, wi_hbm,
    out_ref, wg_ref, rg_ref,
    xv, dy, xg, wo, wi, acc, gbuf, rbuf, sbuf,
    ends, leaves, grown, faded, fades, grows, intra, decays, mixes, lrow, lcol, etot, wacc,
    end_own, leave_own, s_in, s_out, g_in, g_out,
    x_sem, wo_sem, wi_sem, ag_ss, ag_sr, rs_ss, rs_sr, st_ss, st_sr, gr_ss, gr_sr,
):
    rows, feats = grad_ref.shape
    heads = ld_ref.shape[0]
    width = wo.shape[1]
    cols = out_ref.shape[1]
    nstate = b_ref.shape[1]
    hp = width // heads
    q = CHUNK
    nc = rows // q
    pairs = heads // 2
    n = nhead
    half = rows // 2
    piece = half // SUB

    def x_copy():
        return pltpu.make_async_copy(x_hbm, xv, x_sem)

    def wo_copy(b):
        at = pl.multiple_of(b * feats, 128)
        return pltpu.make_async_copy(wo_hbm.at[:, pl.ds(at, feats)], wo.at[b], wo_sem.at[b])

    def wi_copy(b):
        return pltpu.make_async_copy(wi_hbm.at[pl.ds(b * cols, cols)], wi.at[b], wi_sem.at[b])

    x_copy().start()
    for b in range(n):
        wo_copy(b).start()

    me = lax.axis_index("head")
    place = ring_index(me, n)
    right = ring_index(lax.rem(place + 1, n), n)
    left = ring_index(lax.rem(place + n - 1, n), n)
    ctx = lax.axis_index("ctx")
    ahead = jnp.minimum(ctx + 1, nctx - 1)
    behind = jnp.maximum(ctx - 1, 0)

    barrier = pltpu.get_barrier_semaphore()
    for target in (left, right):
        pl.semaphore_signal(barrier, inc=1, device_id={"head": target}, device_id_type=MESH)

    @pl.when(ctx < nctx - 1)
    def _():
        pl.semaphore_signal(barrier, inc=1, device_id={"ctx": ahead}, device_id_type=MESH)

    @pl.when(ctx > 0)
    def _():
        pl.semaphore_signal(barrier, inc=1, device_id={"ctx": behind}, device_id_type=MESH)

    pl.semaphore_wait(
        barrier, 2 + jnp.where(ctx > 0, 1, 0) + jnp.where(ctx < nctx - 1, 1, 0)
    )

    def span(d, g):
        return pl.ds(d * half + g * piece, piece)

    def ag_copy(s, d, g):
        src = grad_ref.at[span(d, g)] if s == 0 else gbuf.at[s - 1, span(d, g)]
        return pltpu.make_async_remote_copy(
            src_ref=src,
            dst_ref=gbuf.at[s, span(d, g)],
            send_sem=ag_ss.at[s, d, g],
            recv_sem=ag_sr.at[s, d, g],
            device_id={"head": right if d == 0 else left},
            device_id_type=MESH,
        )

    for g in range(SUB):
        for d in range(2):
            ag_copy(0, d, g).start()
    for b in range(n):
        wi_copy(b).start()

    @pl.when(ctx == 0)
    def _():
        s_in[...] = jnp.zeros_like(s_in)

    @pl.when(ctx == nctx - 1)
    def _():
        g_in[...] = jnp.zeros_like(g_in)

    first = lax.broadcasted_iota(jnp.int32, (q, q), 0)
    second = lax.broadcasted_iota(jnp.int32, (q, q), 1)
    low = lax.broadcasted_iota(jnp.int32, (q, 2 * hp), 1) < hp

    def scaled(factor, state):
        out = factor[:, None, :] * state.reshape(heads, hp, nstate)
        return out.reshape(width, nstate)

    hstep = heads // PIECES
    step = width // PIECES

    def relay(own, got, out, sends, recvs, target, receives, passes):
        def copy(i):
            at = pl.ds(i * step, step)
            return pltpu.make_async_remote_copy(
                src_ref=out.at[at],
                dst_ref=got.at[at],
                send_sem=sends.at[i],
                recv_sem=recvs.at[i],
                device_id={"ctx": target},
                device_id_type=MESH,
            )

        def run():
            for i in range(PIECES):
                at = pl.ds(i * step, step)

                @pl.when(receives)
                def _():
                    copy(i).wait_recv()

                @pl.when(passes)
                def _():
                    factor = etot[nc, i * hstep : (i + 1) * hstep, :]
                    come = got[at, :].astype(F32).reshape(hstep, hp, nstate)
                    come = (factor[:, None, :] * come).reshape(step, nstate)
                    out[at, :] = (own[at, :] + come).astype(BF16)
                    copy(i).start()

        def finish():
            @pl.when(passes)
            def _():
                for i in range(PIECES):
                    copy(i).wait_send()

        return run, finish

    run_s, finish_s = relay(
        end_own, s_in, s_out, st_ss, st_sr, ahead, ctx > 0, ctx < nctx - 1
    )
    run_g, finish_g = relay(
        leave_own, g_in, g_out, gr_ss, gr_sr, behind, ctx < nctx - 1, ctx > 0
    )

    x_copy().wait()
    upto = (first <= second).astype(F32)
    downto = (first >= second).astype(F32)
    after = (first < second).astype(F32)
    ones = jnp.ones((q, nstate), F32)
    head_at = lax.broadcasted_iota(jnp.int32, (heads, width), 0) * hp
    lane_at = lax.broadcasted_iota(jnp.int32, (heads, width), 1)
    spread = ((lane_at >= head_at) & (lane_at < head_at + hp)).astype(BF16)
    total = jnp.zeros((heads, nstate), F32)
    for k in range(nc):
        at = pl.ds(k * q, q)
        ldk = ld_ref[:, k * q : (k + 1) * q]
        lrow[k] = mm(ldk, upto, precision=HIGH)
        lc = mm(downto, ldk, NT, HIGH)
        lcol[k] = lc
        whole = mm(ldk, ones, precision=HIGH)
        total = total + whole
        etot[k] = jnp.exp(whole)
        fade = mm(jnp.exp(mm(after, ldk, NT, HIGH)).astype(BF16), spread)
        fades[at, :] = fade.astype(BF16)
        grows[at, :] = mm(jnp.exp(lc).astype(BF16), spread).astype(BF16)
        fx = (xv[at, :].astype(F32) * fade).astype(BF16)
        faded[at, :] = fx
        ends[k] = mm(fx, b_ref[at, :], TN)
    etot[nc] = jnp.exp(total)
    state = ends[0]
    for k in range(1, nc):
        state = scaled(etot[k], state) + ends[k]
    end_own[...] = state

    def prepare(k):
        at = pl.ds(pl.multiple_of(k * q, q), q)
        score = mm(b_ref[at, :], c_ref[at, :], NT)
        score2 = jnp.concatenate([score, score], axis=1)
        keep = jnp.concatenate([first <= second, first <= second], axis=1)
        colk = lcol[k]
        for j in range(pairs):
            d0 = lrow[k, 2 * j : 2 * j + 1, :] - colk[:, 2 * j : 2 * j + 1]
            d1 = lrow[k, 2 * j + 1 : 2 * j + 2, :] - colk[:, 2 * j + 1 : 2 * j + 2]
            decay = jnp.exp(jnp.where(keep, jnp.concatenate([d0, d1], axis=1), -1e30))
            decays[k, j] = decay
            mixes[k, j] = (decay * score2).astype(BF16)

    def owner(s, d):
        return ring_index(lax.rem(place + (n - s if d == 0 else s), n), n)

    def accumulate(s, d, row0, count):
        own = owner(s, d)
        src = grad_ref if s == 0 else gbuf.at[s - 1]

        @pl.loop(0, width // TILE)
        def _(j):
            lanes = pl.ds(pl.multiple_of(j * TILE, TILE), TILE)
            part = mm(src[pl.ds(row0, count), :], wo[own, lanes, :], NT)
            at = (pl.ds(row0, count), lanes)
            if s == 0:
                acc[at] = part
            elif s == n - 1:
                dy[at] = (acc[at] + part).astype(dy.dtype)
            else:
                acc[at] += part

    for b in range(n):
        wo_copy(b).wait()
    at_s = (ctx * (n - 1)) // nctx
    for s in range(n - 1):
        if s > 0:
            for g in range(SUB):
                for d in range(2):
                    ag_copy(s - 1, d, g).wait_recv()
                    ag_copy(s, d, g).start()
        for d in range(2):
            accumulate(s, d, d * half, half)
        pl.when(at_s == s)(run_s)
        if s > 0:
            lo, hi = (nc * (s - 1)) // (n - 2), (nc * s) // (n - 2)
            if hi > lo:
                pl.loop(lo, hi)(prepare)
    for g in range(SUB):
        for d in range(2):
            ag_copy(n - 2, d, g).wait_recv()
            accumulate(n - 1, d, d * half + g * piece, piece)

    for k in range(nc):
        at = pl.ds(k * q, q)
        gd = dy[at, :] * grows[at, :]
        grown[at, :] = gd
        leaves[k] = mm(gd, c_ref[at, :], TN)
    grad = leaves[nc - 1]
    for k in range(nc - 2, -1, -1):
        grad = leaves[k] + scaled(etot[k], grad)
    leave_own[...] = grad

    points = POINTS * nc
    at_g = ((nctx - 1 - ctx) * points) // nctx

    @pl.loop(0, nc)
    def _(k):
        at = pl.ds(pl.multiple_of(k * q, q), q)
        for j in range(pairs):
            if j % (pairs // POINTS) == 0:
                pl.when(k * POINTS + j // (pairs // POINTS) == at_g)(run_g)
            lanes = slice(j * 2 * hp, (j + 1) * 2 * hp)
            dyp = dy[at, lanes]
            none = jnp.zeros_like(dyp)
            dyst = jnp.concatenate([jnp.where(low, dyp, none), jnp.where(low, none, dyp)], axis=0)
            mixed = decays[k, j] * mm(xv[at, lanes], dyst, NT)
            if j == 0:
                wacc[...] = mixed
            else:
                wacc[...] += mixed
            intra[at, lanes] = mm(mixes[k, j], dyst)
        both = wacc[...]
        weight = (both[:, :q] + both[:, q:]).astype(BF16)
        wg_ref[at, :] = mm(weight, c_ref[at, :])
        rg_ref[at, :] = mm(weight, b_ref[at, :], TN)

    state = s_in[...].astype(F32)
    for k in range(nc):
        at = pl.ds(k * q, q)
        rg_ref[at, :] += mm(grown[at, :], state.astype(BF16))
        if k < nc - 1:
            state = scaled(etot[k], state) + ends[k]
    for b in range(n):
        wi_copy(b).wait()
    grad = g_in[...].astype(F32)
    for k in range(nc - 1, -1, -1):
        at = pl.ds(k * q, q)
        gb = grad.astype(BF16)
        inter = mm(b_ref[at, :], gb, NT)
        xg[at, :] = (intra[at, :] + fades[at, :].astype(F32) * inter).astype(BF16)
        wg_ref[at, :] += mm(faded[at, :], gb)
        if k > 0:
            grad = leaves[k] + scaled(etot[k], grad)

    def rs_copy(s, d, g):
        return pltpu.make_async_remote_copy(
            src_ref=sbuf.at[s, span(d, g)],
            dst_ref=rbuf.at[s, span(d, g)],
            send_sem=rs_ss.at[s, d, g],
            recv_sem=rs_sr.at[s, d, g],
            device_id={"head": right if d == 0 else left},
            device_id_type=MESH,
        )

    def term(s, d, row0, count, dest_ref):
        if d == 0:
            dest = ring_index(lax.rem(place + 2 * n - 1 - s, n), n)
        else:
            dest = ring_index(lax.rem(place + 1 + s, n), n)
        at = pl.ds(row0, count)

        @pl.loop(0, cols // TILE)
        def _(j):
            lanes = pl.ds(pl.multiple_of(j * TILE, TILE), TILE)
            part = mm(xg[at, :], wi[dest, lanes, :], NT)
            dest_ref[at, lanes] = part.astype(dest_ref.dtype)

    for g in range(SUB):
        for d in range(2):
            term(0, d, d * half + g * piece, piece, sbuf.at[0])
            rs_copy(0, d, g).start()
    for s in range(1, n):
        for d in range(2):
            term(s, d, d * half, half, acc)
        for g in range(SUB):
            for d in range(2):
                rs_copy(s - 1, d, g).wait_recv()
                at = span(d, g)
                part = acc[at, :cols] + rbuf[s - 1, at, :].astype(F32)
                if s == n - 1:
                    out_ref[at, :] = part.astype(out_ref.dtype)
                else:
                    sbuf[s, at, :] = part.astype(BF16)
                    rs_copy(s, d, g).start()
    for s in range(n - 1):
        for g in range(SUB):
            for d in range(2):
                ag_copy(s, d, g).wait_send()
                rs_copy(s, d, g).wait_send()
    finish_s()
    finish_g()


def per_device(
    nctx, nhead, ssd_input, log_decay, write_proj, read_proj, in_weight, out_weight, out_grad
):
    rows, width = ssd_input.shape
    nstate = write_proj.shape[2]
    heads = log_decay.shape[0]
    feats = out_grad.shape[1]
    n = nhead
    cols = in_weight.shape[0] // n
    nc = rows // CHUNK
    pairs = heads // 2
    vm = pl.BlockSpec(memory_space=pltpu.VMEM)
    hbm = pl.BlockSpec(memory_space=pl.ANY)
    dma = pltpu.SemaphoreType.DMA
    state = pltpu.VMEM((width, nstate), BF16)
    input_grad, write_grad, read_grad = pl.pallas_call(
        functools.partial(layer_kernel, nctx, nhead),
        name="layer",
        out_shape=(
            jax.ShapeDtypeStruct((rows, cols), BF16),
            jax.ShapeDtypeStruct((rows, nstate), F32),
            jax.ShapeDtypeStruct((rows, nstate), F32),
        ),
        in_specs=[vm, hbm, vm, vm, vm, hbm, hbm],
        out_specs=(vm, vm, vm),
        scratch_shapes=[
            pltpu.VMEM((rows, width), BF16),
            pltpu.VMEM((rows, width), BF16),
            pltpu.VMEM((rows, width), BF16),
            pltpu.VMEM((n, width, feats), BF16),
            pltpu.VMEM((n, cols, width), BF16),
            pltpu.VMEM((rows, max(width, cols)), F32),
            pltpu.VMEM((n - 1, rows, feats), BF16),
            pltpu.VMEM((n - 1, rows, cols), BF16),
            pltpu.VMEM((n - 1, rows, cols), BF16),
            pltpu.VMEM((nc, width, nstate), F32),
            pltpu.VMEM((nc, width, nstate), F32),
            pltpu.VMEM((rows, width), BF16),
            pltpu.VMEM((rows, width), BF16),
            pltpu.VMEM((rows, width), BF16),
            pltpu.VMEM((rows, width), BF16),
            pltpu.VMEM((rows, width), F32),
            pltpu.VMEM((nc, pairs, CHUNK, 2 * CHUNK), F32),
            pltpu.VMEM((nc, pairs, CHUNK, 2 * CHUNK), BF16),
            pltpu.VMEM((nc, heads, CHUNK), F32),
            pltpu.VMEM((nc, CHUNK, heads), F32),
            pltpu.VMEM((nc + 1, heads, nstate), F32),
            pltpu.VMEM((CHUNK, 2 * CHUNK), F32),
            pltpu.VMEM((width, nstate), F32),
            pltpu.VMEM((width, nstate), F32),
            state, state, state, state,
            dma, dma((n,)), dma((n,)),
            dma((n - 1, 2, SUB)), dma((n - 1, 2, SUB)),
            dma((n - 1, 2, SUB)), dma((n - 1, 2, SUB)),
            dma((PIECES,)), dma((PIECES,)), dma((PIECES,)), dma((PIECES,)),
        ],
        compiler_params=pltpu.CompilerParams(
            collective_id=0, has_side_effects=True, vmem_limit_bytes=VMEM_LIMIT
        ),
    )(
        out_grad,
        ssd_input,
        log_decay,
        write_proj.reshape(rows, nstate),
        read_proj.reshape(rows, nstate),
        out_weight,
        in_weight,
    )
    return (input_grad, write_grad.reshape(rows, 1, nstate), read_grad.reshape(rows, 1, nstate))


def solution(mesh):
    placed = (
        P("ctx", "head"),
        P("head", "ctx"),
        P("ctx", "head", None),
        P("ctx", "head", None),
        P(None, "head"),
        P("head", None),
        P("ctx", "head"),
    )
    return jax.shard_map(
        functools.partial(per_device, mesh.shape["ctx"], mesh.shape["head"]),
        mesh=mesh,
        in_specs=placed,
        out_specs=(P("ctx", "head"), P("ctx", "head", None), P("ctx", "head", None)),
        check_vma=False,
    )
```

```python
import functools

import jax
import jax.numpy as jnp
from jax import lax
from jax.experimental import pallas as pl
from jax.experimental.pallas import tpu as pltpu
from jax.sharding import PartitionSpec as P

CHUNK = 128
SUB = 2
PIECES = 8
POINTS = 2
TILE = 256
MESH = pl.DeviceIdType.MESH
HIGH = lax.Precision.HIGHEST
F32 = jnp.float32
BF16 = jnp.bfloat16
NT = (((1,), (1,)), ((), ()))
TN = (((0,), (0,)), ((), ()))
VMEM_LIMIT = 60 * 1024 * 1024


def mm(a, b, dims=(((1,), (0,)), ((), ())), precision=None):
    return lax.dot_general(a, b, dims, precision=precision, preferred_element_type=F32)


def ring_index(place, n):
    half = n // 2
    return jnp.where(place < half, place, n + half - 1 - place)


def layer_kernel(
    nctx, nhead, grad_ref, x_hbm, ld_ref, b_ref, c_ref, wo_hbm, wi_hbm,
    out_ref, wg_ref, rg_ref,
    xv, dy, xg, wo, wi, acc, gbuf, rbuf, sbuf,
    ends, leaves, grown, faded, fades, grows, intra, decays, mixes, lrow, lcol, etot, wacc,
    end_own, leave_own, s_in, s_out, g_in, g_out,
    x_sem, wo_sem, wi_sem, ag_ss, ag_sr, rs_ss, rs_sr, st_ss, st_sr, gr_ss, gr_sr,
):
    rows, feats = grad_ref.shape
    heads = ld_ref.shape[0]
    width = wo.shape[1]
    cols = out_ref.shape[1]
    nstate = b_ref.shape[1]
    hp = width // heads
    q = CHUNK
    nc = rows // q
    pairs = heads // 2
    n = nhead
    half = rows // 2
    piece = half // SUB

    def x_copy():
        return pltpu.make_async_copy(x_hbm, xv, x_sem)

    def wo_copy(b):
        at = pl.multiple_of(b * feats, 128)
        return pltpu.make_async_copy(wo_hbm.at[:, pl.ds(at, feats)], wo.at[b], wo_sem.at[b])

    def wi_copy(b):
        return pltpu.make_async_copy(wi_hbm.at[pl.ds(b * cols, cols)], wi.at[b], wi_sem.at[b])

    x_copy().start()
    for b in range(n):
        wo_copy(b).start()

    me = lax.axis_index("head")
    place = ring_index(me, n)
    right = ring_index(lax.rem(place + 1, n), n)
    left = ring_index(lax.rem(place + n - 1, n), n)
    ctx = lax.axis_index("ctx")
    ahead = jnp.minimum(ctx + 1, nctx - 1)
    behind = jnp.maximum(ctx - 1, 0)

    barrier = pltpu.get_barrier_semaphore()
    for target in (left, right):
        pl.semaphore_signal(barrier, inc=1, device_id={"head": target}, device_id_type=MESH)

    @pl.when(ctx < nctx - 1)
    def _():
        pl.semaphore_signal(barrier, inc=1, device_id={"ctx": ahead}, device_id_type=MESH)

    @pl.when(ctx > 0)
    def _():
        pl.semaphore_signal(barrier, inc=1, device_id={"ctx": behind}, device_id_type=MESH)

    pl.semaphore_wait(
        barrier, 2 + jnp.where(ctx > 0, 1, 0) + jnp.where(ctx < nctx - 1, 1, 0)
    )

    def span(d, g):
        return pl.ds(d * half + g * piece, piece)

    def ag_copy(s, d, g):
        src = grad_ref.at[span(d, g)] if s == 0 else gbuf.at[s - 1, span(d, g)]
        return pltpu.make_async_remote_copy(
            src_ref=src,
            dst_ref=gbuf.at[s, span(d, g)],
            send_sem=ag_ss.at[s, d, g],
            recv_sem=ag_sr.at[s, d, g],
            device_id={"head": right if d == 0 else left},
            device_id_type=MESH,
        )

    for g in range(SUB):
        for d in range(2):
            ag_copy(0, d, g).start()
    for b in range(n):
        wi_copy(b).start()

    @pl.when(ctx == 0)
    def _():
        s_in[...] = jnp.zeros_like(s_in)

    @pl.when(ctx == nctx - 1)
    def _():
        g_in[...] = jnp.zeros_like(g_in)

    first = lax.broadcasted_iota(jnp.int32, (q, q), 0)
    second = lax.broadcasted_iota(jnp.int32, (q, q), 1)
    low = lax.broadcasted_iota(jnp.int32, (q, 2 * hp), 1) < hp

    def scaled(factor, state):
        out = factor[:, None, :] * state.reshape(heads, hp, nstate)
        return out.reshape(width, nstate)

    hstep = heads // PIECES
    step = width // PIECES

    def relay(own, got, out, sends, recvs, target, receives, passes):
        def copy(i):
            at = pl.ds(i * step, step)
            return pltpu.make_async_remote_copy(
                src_ref=out.at[at],
                dst_ref=got.at[at],
                send_sem=sends.at[i],
                recv_sem=recvs.at[i],
                device_id={"ctx": target},
                device_id_type=MESH,
            )

        def run():
            for i in range(PIECES):
                at = pl.ds(i * step, step)

                @pl.when(receives)
                def _():
                    copy(i).wait_recv()

                @pl.when(passes)
                def _():
                    factor = etot[nc, i * hstep : (i + 1) * hstep, :]
                    come = got[at, :].astype(F32).reshape(hstep, hp, nstate)
                    come = (factor[:, None, :] * come).reshape(step, nstate)
                    out[at, :] = (own[at, :] + come).astype(BF16)
                    copy(i).start()

        def finish():
            @pl.when(passes)
            def _():
                for i in range(PIECES):
                    copy(i).wait_send()

        return run, finish

    run_s, finish_s = relay(
        end_own, s_in, s_out, st_ss, st_sr, ahead, ctx > 0, ctx < nctx - 1
    )
    run_g, finish_g = relay(
        leave_own, g_in, g_out, gr_ss, gr_sr, behind, ctx < nctx - 1, ctx > 0
    )

    x_copy().wait()
    upto = (first <= second).astype(F32)
    downto = (first >= second).astype(F32)
    after = (first < second).astype(F32)
    ones = jnp.ones((q, nstate), F32)
    head_at = lax.broadcasted_iota(jnp.int32, (heads, width), 0) * hp
    lane_at = lax.broadcasted_iota(jnp.int32, (heads, width), 1)
    spread = ((lane_at >= head_at) & (lane_at < head_at + hp)).astype(BF16)
    total = jnp.zeros((heads, nstate), F32)
    for k in range(nc):
        at = pl.ds(k * q, q)
        ldk = ld_ref[:, k * q : (k + 1) * q]
        lrow[k] = mm(ldk, upto, precision=HIGH)
        lc = mm(downto, ldk, NT, HIGH)
        lcol[k] = lc
        whole = mm(ldk, ones, precision=HIGH)
        total = total + whole
        etot[k] = jnp.exp(whole)
        fade = mm(jnp.exp(mm(after, ldk, NT, HIGH)).astype(BF16), spread)
        fades[at, :] = fade.astype(BF16)
        grows[at, :] = mm(jnp.exp(lc).astype(BF16), spread).astype(BF16)
        fx = (xv[at, :].astype(F32) * fade).astype(BF16)
        faded[at, :] = fx
        ends[k] = mm(fx, b_ref[at, :], TN)
    etot[nc] = jnp.exp(total)
    state = ends[0]
    for k in range(1, nc):
        state = scaled(etot[k], state) + ends[k]
    end_own[...] = state

    def prepare(k):
        at = pl.ds(pl.multiple_of(k * q, q), q)
        score = mm(b_ref[at, :], c_ref[at, :], NT)
        score2 = jnp.concatenate([score, score], axis=1)
        keep = jnp.concatenate([first <= second, first <= second], axis=1)
        colk = lcol[k]
        for j in range(pairs):
            d0 = lrow[k, 2 * j : 2 * j + 1, :] - colk[:, 2 * j : 2 * j + 1]
            d1 = lrow[k, 2 * j + 1 : 2 * j + 2, :] - colk[:, 2 * j + 1 : 2 * j + 2]
            decay = jnp.exp(jnp.where(keep, jnp.concatenate([d0, d1], axis=1), -1e30))
            decays[k, j] = decay
            mixes[k, j] = (decay * score2).astype(BF16)

    def owner(s, d):
        return ring_index(lax.rem(place + (n - s if d == 0 else s), n), n)

    def accumulate(s, d, row0, count):
        own = owner(s, d)
        src = grad_ref if s == 0 else gbuf.at[s - 1]

        @pl.loop(0, width // TILE)
        def _(j):
            lanes = pl.ds(pl.multiple_of(j * TILE, TILE), TILE)
            part = mm(src[pl.ds(row0, count), :], wo[own, lanes, :], NT)
            at = (pl.ds(row0, count), lanes)
            if s == 0:
                acc[at] = part
            elif s == n - 1:
                dy[at] = (acc[at] + part).astype(dy.dtype)
            else:
                acc[at] += part

    for b in range(n):
        wo_copy(b).wait()
    at_s = (ctx * (n - 1)) // nctx
    for s in range(n - 1):
        if s > 0:
            for g in range(SUB):
                for d in range(2):
                    ag_copy(s - 1, d, g).wait_recv()
                    ag_copy(s, d, g).start()
        for d in range(2):
            accumulate(s, d, d * half, half)
        pl.when(at_s == s)(run_s)
        if s > 0:
            lo, hi = (nc * (s - 1)) // (n - 2), (nc * s) // (n - 2)
            if hi > lo:
                pl.loop(lo, hi)(prepare)
    for g in range(SUB):
        for d in range(2):
            ag_copy(n - 2, d, g).wait_recv()
            accumulate(n - 1, d, d * half + g * piece, piece)

    for k in range(nc):
        at = pl.ds(k * q, q)
        gd = dy[at, :] * grows[at, :]
        grown[at, :] = gd
        leaves[k] = mm(gd, c_ref[at, :], TN)
    grad = leaves[nc - 1]
    for k in range(nc - 2, -1, -1):
        grad = leaves[k] + scaled(etot[k], grad)
    leave_own[...] = grad

    points = POINTS * nc
    at_g = ((nctx - 1 - ctx) * points) // nctx

    @pl.loop(0, nc)
    def _(k):
        at = pl.ds(pl.multiple_of(k * q, q), q)
        for j in range(pairs):
            if j % (pairs // POINTS) == 0:
                pl.when(k * POINTS + j // (pairs // POINTS) == at_g)(run_g)
            lanes = slice(j * 2 * hp, (j + 1) * 2 * hp)
            dyp = dy[at, lanes]
            none = jnp.zeros_like(dyp)
            dyst = jnp.concatenate([jnp.where(low, dyp, none), jnp.where(low, none, dyp)], axis=0)
            mixed = decays[k, j] * mm(xv[at, lanes], dyst, NT)
            if j == 0:
                wacc[...] = mixed
            else:
                wacc[...] += mixed
            intra[at, lanes] = mm(mixes[k, j], dyst)
        both = wacc[...]
        weight = (both[:, :q] + both[:, q:]).astype(BF16)
        wg_ref[at, :] = mm(weight, c_ref[at, :])
        rg_ref[at, :] = mm(weight, b_ref[at, :], TN)

    for b in range(n):
        wi_copy(b).wait()
    grad = g_in[...].astype(F32)
    for k in range(nc - 1, -1, -1):
        at = pl.ds(k * q, q)
        gb = grad.astype(BF16)
        inter = mm(b_ref[at, :], gb, NT)
        xg[at, :] = (intra[at, :] + fades[at, :].astype(F32) * inter).astype(BF16)
        wg_ref[at, :] += mm(faded[at, :], gb)
        if k > 0:
            grad = leaves[k] + scaled(etot[k], grad)

    def rs_copy(s, d, g):
        return pltpu.make_async_remote_copy(
            src_ref=sbuf.at[s, span(d, g)],
            dst_ref=rbuf.at[s, span(d, g)],
            send_sem=rs_ss.at[s, d, g],
            recv_sem=rs_sr.at[s, d, g],
            device_id={"head": right if d == 0 else left},
            device_id_type=MESH,
        )

    def term(s, d, row0, count, dest_ref):
        if d == 0:
            dest = ring_index(lax.rem(place + 2 * n - 1 - s, n), n)
        else:
            dest = ring_index(lax.rem(place + 1 + s, n), n)
        at = pl.ds(row0, count)

        @pl.loop(0, cols // TILE)
        def _(j):
            lanes = pl.ds(pl.multiple_of(j * TILE, TILE), TILE)
            part = mm(xg[at, :], wi[dest, lanes, :], NT)
            dest_ref[at, lanes] = part.astype(dest_ref.dtype)

    for g in range(SUB):
        for d in range(2):
            term(0, d, d * half + g * piece, piece, sbuf.at[0])
            rs_copy(0, d, g).start()
    state = s_in[...].astype(F32)
    for k in range(nc):
        at = pl.ds(k * q, q)
        rg_ref[at, :] += mm(grown[at, :], state.astype(BF16))
        if k < nc - 1:
            state = scaled(etot[k], state) + ends[k]
    for s in range(1, n):
        for d in range(2):
            term(s, d, d * half, half, acc)
        for g in range(SUB):
            for d in range(2):
                rs_copy(s - 1, d, g).wait_recv()
                at = span(d, g)
                part = acc[at, :cols] + rbuf[s - 1, at, :].astype(F32)
                if s == n - 1:
                    out_ref[at, :] = part.astype(out_ref.dtype)
                else:
                    sbuf[s, at, :] = part.astype(BF16)
                    rs_copy(s, d, g).start()
    for s in range(n - 1):
        for g in range(SUB):
            for d in range(2):
                ag_copy(s, d, g).wait_send()
                rs_copy(s, d, g).wait_send()
    finish_s()
    finish_g()


def per_device(
    nctx, nhead, ssd_input, log_decay, write_proj, read_proj, in_weight, out_weight, out_grad
):
    rows, width = ssd_input.shape
    nstate = write_proj.shape[2]
    heads = log_decay.shape[0]
    feats = out_grad.shape[1]
    n = nhead
    cols = in_weight.shape[0] // n
    nc = rows // CHUNK
    pairs = heads // 2
    vm = pl.BlockSpec(memory_space=pltpu.VMEM)
    hbm = pl.BlockSpec(memory_space=pl.ANY)
    dma = pltpu.SemaphoreType.DMA
    state = pltpu.VMEM((width, nstate), BF16)
    input_grad, write_grad, read_grad = pl.pallas_call(
        functools.partial(layer_kernel, nctx, nhead),
        name="layer",
        out_shape=(
            jax.ShapeDtypeStruct((rows, cols), BF16),
            jax.ShapeDtypeStruct((rows, nstate), F32),
            jax.ShapeDtypeStruct((rows, nstate), F32),
        ),
        in_specs=[vm, hbm, vm, vm, vm, hbm, hbm],
        out_specs=(vm, vm, vm),
        scratch_shapes=[
            pltpu.VMEM((rows, width), BF16),
            pltpu.VMEM((rows, width), BF16),
            pltpu.VMEM((rows, width), BF16),
            pltpu.VMEM((n, width, feats), BF16),
            pltpu.VMEM((n, cols, width), BF16),
            pltpu.VMEM((rows, max(width, cols)), F32),
            pltpu.VMEM((n - 1, rows, feats), BF16),
            pltpu.VMEM((n - 1, rows, cols), BF16),
            pltpu.VMEM((n - 1, rows, cols), BF16),
            pltpu.VMEM((nc, width, nstate), F32),
            pltpu.VMEM((nc, width, nstate), F32),
            pltpu.VMEM((rows, width), BF16),
            pltpu.VMEM((rows, width), BF16),
            pltpu.VMEM((rows, width), BF16),
            pltpu.VMEM((rows, width), BF16),
            pltpu.VMEM((rows, width), F32),
            pltpu.VMEM((nc, pairs, CHUNK, 2 * CHUNK), F32),
            pltpu.VMEM((nc, pairs, CHUNK, 2 * CHUNK), BF16),
            pltpu.VMEM((nc, heads, CHUNK), F32),
            pltpu.VMEM((nc, CHUNK, heads), F32),
            pltpu.VMEM((nc + 1, heads, nstate), F32),
            pltpu.VMEM((CHUNK, 2 * CHUNK), F32),
            pltpu.VMEM((width, nstate), F32),
            pltpu.VMEM((width, nstate), F32),
            state, state, state, state,
            dma, dma((n,)), dma((n,)),
            dma((n - 1, 2, SUB)), dma((n - 1, 2, SUB)),
            dma((n - 1, 2, SUB)), dma((n - 1, 2, SUB)),
            dma((PIECES,)), dma((PIECES,)), dma((PIECES,)), dma((PIECES,)),
        ],
        compiler_params=pltpu.CompilerParams(
            collective_id=0, has_side_effects=True, vmem_limit_bytes=VMEM_LIMIT
        ),
    )(
        out_grad,
        ssd_input,
        log_decay,
        write_proj.reshape(rows, nstate),
        read_proj.reshape(rows, nstate),
        out_weight,
        in_weight,
    )
    return (input_grad, write_grad.reshape(rows, 1, nstate), read_grad.reshape(rows, 1, nstate))


def solution(mesh):
    placed = (
        P("ctx", "head"),
        P("head", "ctx"),
        P("ctx", "head", None),
        P("ctx", "head", None),
        P(None, "head"),
        P("head", None),
        P("ctx", "head"),
    )
    return jax.shard_map(
        functools.partial(per_device, mesh.shape["ctx"], mesh.shape["head"]),
        mesh=mesh,
        in_specs=placed,
        out_specs=(P("ctx", "head"), P("ctx", "head", None), P("ctx", "head", None)),
        check_vma=False,
    )
```
